32 devices in a mesh: groups: 1, local: 32 (over z, y, x, core).
Axes of the slice: x: 2, y: 2, z: 4, core: 2. Of those that a mesh axis runs over, the one named last changes fastest.
Arguments:
- tokens: bfloat16 [2048, 2048], P(('groups', 'local')), may hold values from -6 to 6
- expert_ids: int32 [2048, 2], P(('groups', 'local')), may hold values from 0 to 3, all different within a row; in each aligned block of 64 rows (0 to 63, 64 to 127, ...) at most 48 rows name the same one
- gate_weights: float32 [2048, 2], P(('groups', 'local')), may hold values from 0.2 to 1
- norm_gain: float32 [2048], replicated, may hold values from 0.25 to 1.75
- norm_bias: float32 [2048], replicated, may hold values from -3 to 3
- w_in: bfloat16 [32, 2048, 1024], P('local'), may hold values from -0.125 to 0.125
- b_in: float32 [32, 1024], P('local'), may hold values from -4 to 4
- w_out: bfloat16 [32, 1024, 2048], P('local'), may hold values from -0.0625 to 0.0625
- b_out: float32 [4, 2048], replicated, may hold values from -3 to 3
Outputs:
- mixed_out: bfloat16 [2048, 2048], P(('groups', 'local'))
The draws below stay inside these ranges and needn't reach their ends.
Inputs may be any that keep to these rules, and one draw needn't show every extreme that they name: `expert_ids`: among the 64 tokens of one device, no expert is named by more than 48 pairs, a bound that some block reaches; a token's 2 experts differ.
All inputs are finite; a program needn't handle non-finite values.
Results may differ from the reference program's by a relative error of at most 0.008.
Values may be sent and summed in bfloat16 or wider, within the bound.
A program may use at most 128 MiB of HBM per device.

```python
import math
import jax
import jax.numpy as jnp
import numpy as np
from jax import lax

D = 2048
HID = 8192
HID_DEV = 1024
TOP = 2
TOK_DEV = 64
SPLIT = 8
EXPERTS = 4
TOKENS = 2048
CAP = 48
N_LOCAL = 32


def level_of(stream_key, extent, pieces, least, high):
    loudness, own = 1.0, jax.random.fold_in(stream_key, 6)
    for position, parts in pieces:
        steps = jnp.exp(jax.random.uniform(jax.random.fold_in(own, position), (parts,), jnp.float32, least / len(pieces), high / len(pieces)))
        loudness = loudness * jnp.repeat(steps, extent[position] // parts).reshape([-1 if axis == position else 1 for axis in range(len(extent))])
    return loudness


def deal_out(own_key, own, number, rows, count, top, bound, skew):
    ranking = jax.random.permutation(own_key, count)
    crowded, common = portions_of(count, rows * top, bound, skew, True), portions_of(count, rows * top, bound, skew, False)
    places = jnp.arange(count)

    def named(tallies, offset_by):
        used = int((tallies > 0).sum())
        fixed = max(1, used // 4)
        passed = fixed + (places - fixed + offset_by * (used - fixed)) % max(1, count - fixed)
        return jnp.zeros((count,), jnp.int32).at[ranking[jnp.where(places < fixed, places, passed)]].set(jnp.asarray(tallies, jnp.int32))

    tallies = jnp.where(number % 4 == 0, named(crowded, number // 4), named(common, number - number // 4 - 1))
    mixed = jax.random.permutation(jax.random.fold_in(own, 3), count)
    donor, sink = mixed[0:count // 2 * 2:2], mixed[1:count // 2 * 2:2]
    margin = jnp.minimum(tallies[donor] - 1, bound - tallies[sink]) // 2
    margin = jnp.where((donor == ranking[0]) | (sink == ranking[0]) | (tallies[sink] == 0), 0, jnp.maximum(margin, 0))
    passed = jax.random.randint(jax.random.fold_in(own, 4), (count // 2,), 0, 1 << 20) % (margin + 1)
    tallies = tallies.at[donor].add(-passed).at[sink].add(passed)
    members = jnp.searchsorted(jnp.cumsum(tallies), jnp.arange(rows * top), side="right").astype(jnp.int32)
    table = members.reshape(top, rows).T
    table = table[jax.random.permutation(jax.random.fold_in(own, 1), rows)]
    offset_by = jax.random.randint(jax.random.fold_in(own, 2), (rows, 1), 0, top)
    return jnp.take_along_axis(table, (jnp.arange(top)[None, :] + offset_by) % top, axis=1)


def portions_of(count, total, most, lean, full):
    portions = [(1 << 20) // math.isqrt(grade ** lean) + 1 for grade in range(1, count + 1)]
    largest = most if full else min(most, max(-(-total // count), total * portions[0] // sum(portions)))
    least = 1 if total - largest >= count - 1 else 0
    given, rest = [largest] + [least] * (count - 1), total - largest - least * (count - 1)
    while rest > 0:
        candidates = [i for i in range(1, count) if given[i] < largest] or [i for i in range(1, count) if given[i] < most]
        mass, remaining = sum([portions[i] for i in candidates]), rest
        for i in candidates:
            addition = min(most - given[i], max(1, remaining * portions[i] // mass), rest)
            given[i] = given[i] + addition
            rest = rest - addition
    return np.array(given)


def bell_draw(rng, dims, scale, most, split=(), kind=jnp.bfloat16):
    level = level_of(rng, dims, split, -0.22, 0.18) if split else 1.0
    entries = jax.random.normal(rng, dims, jnp.float32) * scale * level
    return jnp.minimum(jnp.maximum(entries, -most), most).astype(kind)


def setup_inputs(seed: int = 0, part: int = 0) -> dict:
    seeds = jax.random.split(jax.random.key(seed), 10)
    part_keys = jax.random.split(jax.random.fold_in(seeds[9], part), 10)
    tokens = bell_draw(part_keys[0], (TOKENS, D), 1.0, 6.0, ((0, 32),))
    expert_ids_keys = jax.random.split(jax.random.fold_in(part_keys[1], 1), TOKENS // TOK_DEV)
    expert_ids_turns = jax.random.permutation(jax.random.fold_in(part_keys[1], 3), TOKENS // TOK_DEV)
    expert_ids = jax.vmap(lambda own, number: deal_out(jax.random.fold_in(part_keys[1], 2), own, number, TOK_DEV, EXPERTS, TOP, CAP, 2))(expert_ids_keys, expert_ids_turns).reshape((TOKENS, TOP))
    gate_weights = jnp.clip(0.2 + 0.8 * jax.random.uniform(part_keys[2], (TOKENS, TOP), jnp.float32) ** level_of(part_keys[2], (TOKENS, TOP), ((0, 32),), -0.2, 0.2), 0.2, 1.0)
    norm_gain = jnp.clip(1.0 + 0.15 * jax.random.normal(seeds[3], (D,), jnp.float32), 0.25, 1.75)
    norm_bias = bell_draw(seeds[4], (D,), 0.5, 3.0, (), jnp.float32)
    w_in = bell_draw(seeds[5], (EXPERTS * SPLIT, D, HID_DEV), D ** -0.5, 0.125, ((0, 32),))
    b_in = bell_draw(seeds[6], (EXPERTS * SPLIT, HID_DEV), 1.0, 4.0, ((0, 32),), jnp.float32)
    w_out = bell_draw(seeds[7], (EXPERTS * SPLIT, HID_DEV, D), HID ** -0.5, 0.0625, ((0, 32),))
    b_out = bell_draw(seeds[8], (EXPERTS, D), 0.5, 3.0, (), jnp.float32)
    return {"tokens": tokens, "expert_ids": expert_ids, "gate_weights": gate_weights, "norm_gain": norm_gain, "norm_bias": norm_bias, "w_in": w_in, "b_in": b_in, "w_out": w_out, "b_out": b_out}


def layer_norm(values, gain, bias):
    floats = values.astype(jnp.float32)
    row_mean = lax.optimization_barrier(jnp.mean(floats, axis=-1, keepdims=True))
    centered = floats - row_mean
    row_var = lax.optimization_barrier(jnp.mean(centered * centered, axis=-1, keepdims=True))
    return centered * lax.rsqrt(row_var + 1e-05) * gain + bias

def one_expert(operands):
    row_block, weight_in, bias_in, weight_out, bias_out = operands
    hidden = jnp.einsum('rd,sdh->srh', row_block.astype(jnp.float32), weight_in.astype(jnp.float32)) + bias_in[:, None, :]
    hidden = jnp.maximum(hidden, 0.0).astype(jnp.bfloat16)
    partial_value = jnp.einsum('srh,shd->srd', hidden.astype(jnp.float32), weight_out.astype(jnp.float32))
    partial_value = partial_value.astype(jnp.bfloat16).astype(jnp.float32)
    return lax.optimization_barrier(jnp.sum(partial_value, axis=0)) + bias_out[None, :]

def reference(tokens, expert_ids, gate_weights, norm_gain, norm_bias, w_in, b_in, w_out, b_out):
    normed = layer_norm(tokens, norm_gain, norm_bias).astype(jnp.bfloat16)
    flat_ids = expert_ids.reshape(N_LOCAL, TOK_DEV * TOP)
    onehot = (flat_ids[:, :, None] == jnp.arange(EXPERTS, dtype=jnp.int32)[None, None, :]).astype(jnp.int32)
    slot_rank = lax.optimization_barrier(jnp.sum(jnp.cumsum(onehot, axis=1) * onehot, axis=2)) - 1
    device_row = jnp.arange(N_LOCAL, dtype=jnp.int32)[:, None]
    slot_rows = ((device_row * EXPERTS + flat_ids) * CAP + slot_rank).reshape(-1).astype(jnp.int32)
    source_rows = jnp.repeat(normed, TOP, axis=0)
    buffer = jnp.zeros((N_LOCAL * EXPERTS * CAP, D), jnp.bfloat16).at[slot_rows].set(source_rows)
    by_expert = buffer.reshape(N_LOCAL, EXPERTS, CAP, D).transpose(1, 0, 2, 3).reshape(EXPERTS, N_LOCAL * CAP, D)
    split_in = w_in.reshape(EXPERTS, SPLIT, D, HID_DEV)
    split_bias = b_in.reshape(EXPERTS, SPLIT, HID_DEV)
    split_out = w_out.reshape(EXPERTS, SPLIT, HID_DEV, D)
    results = lax.map(one_expert, (by_expert, split_in, split_bias, split_out, b_out))
    returned = results.reshape(EXPERTS, N_LOCAL, CAP, D).transpose(1, 0, 2, 3).reshape(N_LOCAL * EXPERTS * CAP, D)
    picked = returned[slot_rows].reshape(TOKENS, TOP, D)
    mixed_out = tokens.astype(jnp.float32) + lax.optimization_barrier(jnp.sum(gate_weights[:, :, None] * picked, axis=1))
    return mixed_out.astype(jnp.bfloat16)
```

```python
import functools

import jax
import jax.numpy as jnp
from jax import lax
from jax.experimental import pallas as pl
from jax.experimental.pallas import tpu as pltpu
from jax.sharding import PartitionSpec as P

MESH = pl.DeviceIdType.MESH
F32 = jnp.float32
BF16 = jnp.bfloat16
ZIN, OWN_A, REST_A, OWN_B, REST_B, OWN_P, FWD_B, FWD_P1, FWD_P2, FWD_P3, FWD_A = range(11)
PAIR, DIAG, ONE, TWO, BACK = 11, 13, 15, 17, 19
KINDS = 21


def xor_with(value, fixed, limit):
    out, bit = 0, 1
    while bit < limit:
        digit = lax.rem(lax.div(value, bit), 2)
        out = out + bit * ((1 - digit) if fixed & bit else digit)
        bit *= 2
    return out


def kernel(
    experts, cap, tokens_ref, idst_ref, gatest_ref, gain_ref, bias_ref, b_in_ref, b_out_ref,
    w_in_hbm, w_out_hbm, out_ref, w_in, w_out, rows, outbox, hidden, part, pair, diag, from_b, from_a,
    sums, back, returned, load_sems, send_sems, recv_sems,
):
    tok, width = tokens_ref.shape
    hid = hidden.shape[1]
    half = width // 2
    shared = 8
    me = lax.axis_index("local")
    plane = lax.div(me, shared)
    seat = lax.rem(me, shared)
    core = lax.rem(seat, 2)
    base = plane * shared
    seat_x = seat + 2 - 4 * lax.rem(lax.div(seat, 2), 2)
    seat_y = seat + 4 - 8 * lax.div(seat, 4)
    mate = base + seat + 1 - 2 * core
    near_a = base + seat_x + core * (seat_y - seat_x)
    near_b = base + seat_y + core * (seat_x - seat_y)
    planes = [xor_with(plane, j, experts) for j in range(experts)]
    others = [planes[j] * shared + seat for j in range(experts)]

    loads = [
        pltpu.make_async_copy(w_in_hbm.at[0], w_in, load_sems.at[0]),
        pltpu.make_async_copy(w_out_hbm.at[0], w_out, load_sems.at[1]),
    ]
    for load in loads:
        load.start()

    barrier = pltpu.get_barrier_semaphore()
    partners = [mate, near_a, near_b] + others[1:]
    for partner in partners:
        pl.semaphore_signal(barrier, inc=1, device_id={"local": partner}, device_id_type=MESH)

    def chunk(j, q, count=1):
        return rows.at[j, pl.ds(q * cap, count * cap)]

    def piece(j, q, at):
        return rows.at[j, pl.ds(q * cap, cap), at]

    def copy(j, kind, src, dst, target):
        return pltpu.make_async_remote_copy(
            src_ref=src, dst_ref=dst, send_sem=send_sems.at[j * KINDS + kind],
            recv_sem=recv_sems.at[j * KINDS + kind], device_id={"local": target}, device_id_type=MESH,
        )

    copies = {}
    for j in range(experts):
        if j:
            copies[j, ZIN] = copy(j, ZIN, outbox.at[j], chunk(j, 0), others[j])
        low, high = pl.ds(0, half), pl.ds(half, half)
        copies[j, OWN_A] = copy(j, OWN_A, piece(j, 0, low), piece(j, 1, low), near_a)
        copies[j, REST_A] = copy(j, REST_A, piece(j, 0, high), piece(j, 1, high), near_a)
        copies[j, OWN_B] = copy(j, OWN_B, piece(j, 0, high), piece(j, 2, high), near_b)
        copies[j, REST_B] = copy(j, REST_B, piece(j, 0, low), piece(j, 2, low), near_b)
        copies[j, OWN_P] = copy(j, OWN_P, chunk(j, 0), chunk(j, 4), mate)
        copies[j, FWD_B] = copy(j, FWD_B, piece(j, 1, low), piece(j, 3, low), near_b)
        copies[j, FWD_A] = copy(j, FWD_A, piece(j, 2, high), piece(j, 3, high), near_a)
        copies[j, FWD_P1] = copy(j, FWD_P1, chunk(j, 1), chunk(j, 5), mate)
        copies[j, FWD_P2] = copy(j, FWD_P2, chunk(j, 2), chunk(j, 6), mate)
        copies[j, FWD_P3] = copy(j, FWD_P3, chunk(j, 3), chunk(j, 7), mate)
        for h in range(2):
            at = pl.ds(h * half, half)
            every = pl.ds(0, cap)
            copies[j, PAIR + h] = copy(
                j, PAIR + h, part.at[j, pl.ds(4 * cap, 4 * cap), at], pair.at[j, pl.ds(0, 4 * cap), at], mate
            )
            via, out = (near_a, near_b) if h else (near_b, near_a)
            at_via, at_out = (from_a, from_b) if h else (from_b, from_a)
            copies[j, DIAG + h] = copy(j, DIAG + h, sums.at[j, 0, every, at], diag.at[j, every, at], via)
            copies[j, ONE + h] = copy(j, ONE + h, sums.at[j, 1, every, at], at_via.at[j, every, at], via)
            copies[j, TWO + h] = copy(j, TWO + h, sums.at[j, 2, every, at], at_out.at[j, every, at], out)
            if j:
                copies[j, BACK + h] = copy(
                    j, BACK + h, back.at[j, every, at], returned.at[j, every, at], others[j]
                )

    def start(j, *kinds):
        for kind in kinds:
            copies[j, kind].start()

    def arrived(j, *kinds):
        for kind in kinds:
            copies[j, kind].wait_recv()

    row_at = lax.broadcasted_iota(jnp.int32, (tok, tok), 0)
    col_at = lax.broadcasted_iota(jnp.int32, (tok, tok), 1)
    idst = idst_ref[...]
    line = lax.broadcasted_iota(jnp.int32, (16, tok), 0) ^ plane
    first, second = idst[0:1, :] == line, idst[1:2, :] == line
    named_t = jnp.where(first | second, 1.0, 0.0).astype(BF16)
    later = jnp.where(row_at < col_at, 1.0, 0.0).astype(BF16)
    rank_t = jnp.dot(named_t, later, preferred_element_type=F32)

    floats = tokens_ref[...].astype(F32)
    centered = floats - jnp.mean(floats, axis=-1, keepdims=True)
    variance = jnp.mean(centered * centered, axis=-1, keepdims=True)
    normed = (centered * lax.rsqrt(variance + 1e-05) * gain_ref[...] + bias_ref[...]).astype(BF16)
    slot_at = lax.broadcasted_iota(jnp.int32, (cap, tok), 0).astype(F32)
    for j in range(experts):
        take = (rank_t[j : j + 1, :] == slot_at) & (named_t[j : j + 1, :].astype(F32) > 0.5)
        take = jnp.where(take, 1.0, 0.0).astype(BF16)
        block = jnp.dot(take, normed, preferred_element_type=F32).astype(BF16)
        if j:
            outbox[j] = block
        else:
            rows[0, 0:cap, :] = block

    pl.semaphore_wait(barrier, len(partners))
    for j in range(1, min(3, experts)):
        start(j, ZIN)
    start(0, OWN_A, OWN_B, REST_A, REST_B, OWN_P)

    def first_product(j, low, high):
        def tile(n, carry):
            at = pl.ds(pl.multiple_of(n * 256, 256), 256)
            acc = jnp.dot(rows[j], w_in[:, at], preferred_element_type=F32)
            hidden[:, at] = jnp.maximum(acc + b_in_ref[:, at], 0.0).astype(BF16)
            return carry

        lax.fori_loop(low, high, tile, 0)

    def second_product(j, h):
        def tile(n, carry):
            at = pl.ds(pl.multiple_of(n * 256, 256), 256)
            acc = jnp.dot(hidden[...], w_out[:, at], preferred_element_type=F32)
            part[j, :, at] = acc.astype(BF16)
            return carry

        lax.fori_loop(h * half // 256, (h + 1) * half // 256, tile, 0)

    def own(j, q, at):
        span = slice(q * cap, (q + 1) * cap)
        return part[j, span, at].astype(F32) + pair[j, span, at].astype(F32)

    def reduce_a(j, h):
        at = slice(h * half, (h + 1) * half)
        arrived(j, PAIR + h)
        sums[j, 0, :, at] = own(j, 3, at).astype(BF16)
        start(j, DIAG + h)
        sums[j, 1, :, at] = own(j, 2 - h, at).astype(BF16)
        start(j, ONE + h)

    def reduce_b(j, h):
        at = slice(h * half, (h + 1) * half)
        arrived(j, DIAG + h)
        sums[j, 2, :, at] = (own(j, 1 + h, at) + diag[j, :, at].astype(F32)).astype(BF16)
        start(j, TWO + h)

    def reduce_c(j, h):
        at = slice(h * half, (h + 1) * half)
        arrived(j, ONE + h, TWO + h)
        total = (own(j, 0, at) + from_a[j, :, at].astype(F32) + from_b[j, :, at].astype(F32)).astype(BF16)
        if j:
            back[j, :, at] = total
            start(j, BACK + h)
        else:
            returned[0, :, at] = total

    def gather_own(j):
        if j < experts:
            arrived(j, ZIN)
            start(j, OWN_A, OWN_B, REST_A, REST_B, OWN_P)
            if j + 2 < experts:
                start(j + 2, ZIN)

    def gather_next(j):
        if j < experts:
            arrived(j, OWN_A)
            start(j, FWD_B)
            arrived(j, OWN_B)
            start(j, FWD_A)

    def gather_mate(j):
        if j < experts:
            arrived(j, REST_A)
            start(j, FWD_P1)
            arrived(j, REST_B)
            start(j, FWD_P2)

    def gather_last(j):
        if j < experts:
            arrived(j, FWD_B, FWD_A)
            start(j, FWD_P3)

    gather_next(0)
    gather_own(1)
    gather_mate(0)
    gather_last(0)
    tiles = hid // 256
    last = experts - 1
    for j in range(experts):
        if j == 0:
            loads[0].wait()
        else:
            gather_next(j + 1)
        arrived(j, OWN_P, FWD_P1, FWD_P2, FWD_P3)
        if j > 2:
            reduce_a(j - 1, 0)
        first_product(j, 0, tiles // 2)
        if j == 0:
            gather_next(1)
        if j == 2:
            reduce_a(1, 0)
        if j > 2:
            reduce_a(j - 1, 1)
        first_product(j, tiles // 2, tiles)
        if j == 0:
            loads[1].wait()
        gather_own(j + 2)
        if j > 1:
            gather_mate(j + 1)
        if j == 3:
            reduce_b(1, 0)
        second_product(j, 0)
        start(j, PAIR)
        if j > 1:
            gather_last(j + 1)
        else:
            gather_mate(j + 1)
        if j == 2:
            reduce_a(1, 1)
        if j > 2:
            reduce_b(j - 1, 0)
        if j == 3:
            reduce_b(1, 1)
        second_product(j, 1)
        start(j, PAIR + 1)
        if j < 2:
            gather_last(j + 1)
        if j > 2:
            reduce_b(j - 1, 1)
        if j > 3:
            reduce_c(j - 2, 0)
            reduce_c(j - 2, 1)
    reduce_a(last, 0)
    reduce_a(last, 1)
    reduce_c(last - 1, 0)
    reduce_a(0, 0)
    reduce_c(last - 1, 1)
    reduce_b(last, 0)
    reduce_b(last, 1)
    reduce_a(0, 1)
    reduce_c(1, 0)
    reduce_c(1, 1)
    reduce_c(last, 0)
    reduce_b(0, 0)
    reduce_c(last, 1)
    reduce_b(0, 1)
    reduce_c(0, 0)
    reduce_c(0, 1)

    turned = (((1,), (1,)), ((), ()))
    same = jnp.where(row_at == col_at, 1.0, 0.0)
    earlier = jnp.where(col_at < row_at, 1.0, 0.0).astype(BF16)
    named = lax.dot_general(same.astype(BF16), named_t, turned, preferred_element_type=F32)
    rank = lax.dot_general(earlier, named_t, turned, preferred_element_type=F32)
    gatest = gatest_ref[...]
    shares_t = jnp.where(first, gatest[0:1, :], 0.0) + jnp.where(second, gatest[1:2, :], 0.0)
    shares = lax.dot_general(
        same, shares_t, turned, preferred_element_type=F32, precision=lax.Precision.HIGHEST
    )
    place = lax.broadcasted_iota(jnp.int32, (tok, cap), 1).astype(F32)
    gives = []
    for j in range(experts):
        pick = (rank[:, j : j + 1] == place) & (named[:, j : j + 1] > 0.5)
        gives.append(jnp.where(pick, 1.0, 0.0).astype(BF16))
    for j in range(1, experts):
        arrived(j, BACK, BACK + 1)
    for n in range(width // 512):
        at = slice(n * 512, (n + 1) * 512)
        mixed = tokens_ref[:, at].astype(F32)
        for j in range(experts):
            value = jnp.dot(gives[j], returned[j, :, at], preferred_element_type=F32)
            mixed = mixed + shares[:, j : j + 1] * (value + b_out_ref[pl.ds(planes[j], 1), at])
        out_ref[:, at] = mixed.astype(BF16)
    for each in copies.values():
        each.wait_send()


def local(tokens, expert_ids, gate_weights, norm_gain, norm_bias, w_in, b_in, w_out, b_out):
    tok, width = tokens.shape
    top = expert_ids.shape[1]
    devices = lax.axis_size("local")
    experts = b_out.shape[0]
    shared = devices // experts
    hid = b_in.shape[1]
    cap = min(tok, shared * max(1, (3 * tok * top // (2 * experts) + shared - 1) // shared))
    cap = -(-cap // 16) * 16
    vmem = pl.BlockSpec(memory_space=pltpu.VMEM)
    hbm = pl.BlockSpec(memory_space=pl.ANY)
    return pl.pallas_call(
        functools.partial(kernel, experts, cap),
        out_shape=jax.ShapeDtypeStruct((tok, width), BF16),
        in_specs=[vmem] * 7 + [hbm] * 2,
        out_specs=vmem,
        scratch_shapes=[
            pltpu.VMEM((width, hid), BF16),
            pltpu.VMEM((hid, width), BF16),
            pltpu.VMEM((experts, 8 * cap, width), BF16),
            pltpu.VMEM((experts, cap, width), BF16),
            pltpu.VMEM((8 * cap, hid), BF16),
            pltpu.VMEM((experts, 8 * cap, width), BF16),
            pltpu.VMEM((experts, 4 * cap, width), BF16),
            pltpu.VMEM((experts, cap, width), BF16),
            pltpu.VMEM((experts, cap, width), BF16),
            pltpu.VMEM((experts, cap, width), BF16),
            pltpu.VMEM((experts, 3, cap, width), BF16),
            pltpu.VMEM((experts, cap, width), BF16),
            pltpu.VMEM((experts, cap, width), BF16),
            pltpu.SemaphoreType.DMA((2,)),
            pltpu.SemaphoreType.DMA((experts * KINDS,)),
            pltpu.SemaphoreType.DMA((experts * KINDS,)),
        ],
        compiler_params=pltpu.CompilerParams(
            collective_id=0, has_side_effects=True, vmem_limit_bytes=64 * 1024 * 1000
        ),
    )(
        tokens, expert_ids.T, gate_weights.T, norm_gain[None, :], norm_bias[None, :], b_in, b_out, w_in, w_out,
    )


def solution(mesh):
    in_specs = (
        P(("groups", "local"), None),
        P(("groups", "local"), None),
        P(("groups", "local"), None),
        P(),
        P(),
        P("local", None, None),
        P("local", None),
        P("local", None, None),
        P(),
    )
    out_specs = P(("groups", "local"), None)
    return jax.shard_map(local, mesh=mesh, in_specs=in_specs, out_specs=out_specs, check_vma=False)
```

```python
import functools

import jax
import jax.numpy as jnp
from jax import lax
from jax.experimental import pallas as pl
from jax.experimental.pallas import tpu as pltpu
from jax.sharding import PartitionSpec as P

MESH = pl.DeviceIdType.MESH
F32 = jnp.float32
BF16 = jnp.bfloat16
ZIN, OWN_A, REST_A, OWN_B, REST_B, OWN_P, FWD_B, FWD_P1, FWD_P2, FWD_P3, FWD_A = range(11)
PAIR, DIAG, ONE, TWO, BACK = 11, 13, 15, 17, 19
KINDS = 21


def xor_with(value, fixed, limit):
    out, bit = 0, 1
    while bit < limit:
        digit = lax.rem(lax.div(value, bit), 2)
        out = out + bit * ((1 - digit) if fixed & bit else digit)
        bit *= 2
    return out


def kernel(
    experts, cap, tokens_ref, idst_ref, gatest_ref, gain_ref, bias_ref, b_in_ref, b_out_ref,
    w_in_hbm, w_out_hbm, out_ref, w_in, w_out, rows, outbox, hidden, part, pair, diag, from_b, from_a,
    sums, back, returned, load_sems, send_sems, recv_sems,
):
    tok, width = tokens_ref.shape
    hid = hidden.shape[1]
    half = width // 2
    shared = 8
    me = lax.axis_index("local")
    plane = lax.div(me, shared)
    seat = lax.rem(me, shared)
    core = lax.rem(seat, 2)
    base = plane * shared
    seat_x = seat + 2 - 4 * lax.rem(lax.div(seat, 2), 2)
    seat_y = seat + 4 - 8 * lax.div(seat, 4)
    mate = base + seat + 1 - 2 * core
    near_a = base + seat_x + core * (seat_y - seat_x)
    near_b = base + seat_y + core * (seat_x - seat_y)
    planes = [xor_with(plane, j, experts) for j in range(experts)]
    others = [planes[j] * shared + seat for j in range(experts)]

    loads = [
        pltpu.make_async_copy(w_in_hbm.at[0], w_in, load_sems.at[0]),
        pltpu.make_async_copy(w_out_hbm.at[0], w_out, load_sems.at[1]),
    ]
    for load in loads:
        load.start()

    barrier = pltpu.get_barrier_semaphore()
    partners = [mate, near_a, near_b] + others[1:]
    for partner in partners:
        pl.semaphore_signal(barrier, inc=1, device_id={"local": partner}, device_id_type=MESH)

    def chunk(j, q, count=1):
        return rows.at[j, pl.ds(q * cap, count * cap)]

    def piece(j, q, at):
        return rows.at[j, pl.ds(q * cap, cap), at]

    def copy(j, kind, src, dst, target):
        return pltpu.make_async_remote_copy(
            src_ref=src, dst_ref=dst, send_sem=send_sems.at[j * KINDS + kind],
            recv_sem=recv_sems.at[j * KINDS + kind], device_id={"local": target}, device_id_type=MESH,
        )

    copies = {}
    for j in range(experts):
        if j:
            copies[j, ZIN] = copy(j, ZIN, outbox.at[j], chunk(j, 0), others[j])
        low, high = pl.ds(0, half), pl.ds(half, half)
        copies[j, OWN_A] = copy(j, OWN_A, piece(j, 0, low), piece(j, 1, low), near_a)
        copies[j, REST_A] = copy(j, REST_A, piece(j, 0, high), piece(j, 1, high), near_a)
        copies[j, OWN_B] = copy(j, OWN_B, piece(j, 0, high), piece(j, 2, high), near_b)
        copies[j, REST_B] = copy(j, REST_B, piece(j, 0, low), piece(j, 2, low), near_b)
        copies[j, OWN_P] = copy(j, OWN_P, chunk(j, 0), chunk(j, 4), mate)
        copies[j, FWD_B] = copy(j, FWD_B, piece(j, 1, low), piece(j, 3, low), near_b)
        copies[j, FWD_A] = copy(j, FWD_A, piece(j, 2, high), piece(j, 3, high), near_a)
        copies[j, FWD_P1] = copy(j, FWD_P1, chunk(j, 1), chunk(j, 5), mate)
        copies[j, FWD_P2] = copy(j, FWD_P2, chunk(j, 2), chunk(j, 6), mate)
        copies[j, FWD_P3] = copy(j, FWD_P3, chunk(j, 3), chunk(j, 7), mate)
        for h in range(2):
            at = pl.ds(h * half, half)
            every = pl.ds(0, cap)
            copies[j, PAIR + h] = copy(
                j, PAIR + h, part.at[j, pl.ds(4 * cap, 4 * cap), at], pair.at[j, pl.ds(0, 4 * cap), at], mate
            )
            via, out = (near_a, near_b) if h else (near_b, near_a)
            at_via, at_out = (from_a, from_b) if h else (from_b, from_a)
            copies[j, DIAG + h] = copy(j, DIAG + h, sums.at[j, 0, every, at], diag.at[j, every, at], via)
            copies[j, ONE + h] = copy(j, ONE + h, sums.at[j, 1, every, at], at_via.at[j, every, at], via)
            copies[j, TWO + h] = copy(j, TWO + h, sums.at[j, 2, every, at], at_out.at[j, every, at], out)
            if j:
                copies[j, BACK + h] = copy(
                    j, BACK + h, back.at[j, every, at], returned.at[j, every, at], others[j]
                )

    def start(j, *kinds):
        for kind in kinds:
            copies[j, kind].start()

    def arrived(j, *kinds):
        for kind in kinds:
            copies[j, kind].wait_recv()

    row_at = lax.broadcasted_iota(jnp.int32, (tok, tok), 0)
    col_at = lax.broadcasted_iota(jnp.int32, (tok, tok), 1)
    idst = idst_ref[...]
    line = lax.broadcasted_iota(jnp.int32, (16, tok), 0) ^ plane
    first, second = idst[0:1, :] == line, idst[1:2, :] == line
    named_t = jnp.where(first | second, 1.0, 0.0).astype(BF16)
    later = jnp.where(row_at < col_at, 1.0, 0.0).astype(BF16)
    rank_t = jnp.dot(named_t, later, preferred_element_type=F32)

    floats = tokens_ref[...].astype(F32)
    centered = floats - jnp.mean(floats, axis=-1, keepdims=True)
    variance = jnp.mean(centered * centered, axis=-1, keepdims=True)
    normed = (centered * lax.rsqrt(variance + 1e-05) * gain_ref[...] + bias_ref[...]).astype(BF16)
    slot_at = lax.broadcasted_iota(jnp.int32, (cap, tok), 0).astype(F32)
    for j in range(experts):
        take = (rank_t[j : j + 1, :] == slot_at) & (named_t[j : j + 1, :].astype(F32) > 0.5)
        take = jnp.where(take, 1.0, 0.0).astype(BF16)
        block = jnp.dot(take, normed, preferred_element_type=F32).astype(BF16)
        if j:
            outbox[j] = block
        else:
            rows[0, 0:cap, :] = block

    pl.semaphore_wait(barrier, len(partners))
    for j in range(1, min(3, experts)):
        start(j, ZIN)
    start(0, OWN_A, OWN_B, REST_A, REST_B, OWN_P)

    def first_product(j, low, high):
        def tile(n, carry):
            at = pl.ds(pl.multiple_of(n * 256, 256), 256)
            acc = jnp.dot(rows[j], w_in[:, at], preferred_element_type=F32)
            hidden[:, at] = jnp.maximum(acc + b_in_ref[:, at], 0.0).astype(BF16)
            return carry

        lax.fori_loop(low, high, tile, 0)

    def second_product(j, low, high):
        def tile(n, carry):
            at = pl.ds(pl.multiple_of(n * 256, 256), 256)
            acc = jnp.dot(hidden[...], w_out[:, at], preferred_element_type=F32)
            part[j, :, at] = acc.astype(BF16)
            return carry

        lax.fori_loop(low, high, tile, 0)

    def own(j, q, at):
        span = slice(q * cap, (q + 1) * cap)
        return part[j, span, at].astype(F32) + pair[j, span, at].astype(F32)

    def reduce_d(j, h):
        at = slice(h * half, (h + 1) * half)
        arrived(j, PAIR + h)
        sums[j, 0, :, at] = own(j, 3, at).astype(BF16)
        start(j, DIAG + h)

    def reduce_o(j, h):
        at = slice(h * half, (h + 1) * half)
        sums[j, 1, :, at] = own(j, 2 - h, at).astype(BF16)
        start(j, ONE + h)

    def reduce_a(j, h):
        reduce_d(j, h)
        reduce_o(j, h)

    def reduce_b(j, h):
        at = slice(h * half, (h + 1) * half)
        arrived(j, DIAG + h)
        sums[j, 2, :, at] = (own(j, 1 + h, at) + diag[j, :, at].astype(F32)).astype(BF16)
        start(j, TWO + h)

    def reduce_c(j, h):
        at = slice(h * half, (h + 1) * half)
        arrived(j, ONE + h, TWO + h)
        total = (own(j, 0, at) + from_a[j, :, at].astype(F32) + from_b[j, :, at].astype(F32)).astype(BF16)
        if j:
            back[j, :, at] = total
            start(j, BACK + h)
        else:
            returned[0, :, at] = total

    def gather_own(j):
        if j < experts:
            arrived(j, ZIN)
            start(j, OWN_A, OWN_B, REST_A, REST_B, OWN_P)
            if j + 2 < experts:
                start(j + 2, ZIN)

    def gather_next(j):
        if j < experts:
            arrived(j, OWN_A)
            start(j, FWD_B)
            arrived(j, OWN_B)
            start(j, FWD_A)

    def gather_mate(j):
        if j < experts:
            arrived(j, REST_A)
            start(j, FWD_P1)
            arrived(j, REST_B)
            start(j, FWD_P2)

    def gather_last(j):
        if j < experts:
            arrived(j, FWD_B, FWD_A)
            start(j, FWD_P3)

    gather_next(0)
    gather_own(1)
    gather_mate(0)
    gather_last(0)
    tiles = hid // 256
    wide = half // 256
    last = experts - 1
    for j in range(experts):
        if j == 0:
            loads[0].wait()
        if j == 1:
            gather_next(2)
        arrived(j, OWN_P, FWD_P1, FWD_P2, FWD_P3)
        first_product(j, 0, tiles // 2)
        if j != 1:
            gather_next(j + 1)
        else:
            gather_own(3)
        if j > 2:
            reduce_a(j - 1, 1)
        first_product(j, tiles // 2, tiles)
        if j == 0:
            loads[1].wait()
            gather_own(2)
        else:
            gather_mate(j + 1)
        if j == 2:
            reduce_a(1, 0)
        if j == 3:
            reduce_b(1, 0)
        if j > 2:
            reduce_b(j - 1, 0)
        second_product(j, 0, wide)
        start(j, PAIR)
        if j == 0:
            gather_mate(1)
        if j == 1:
            gather_last(2)
            reduce_d(0, 0)
        if j == 2:
            reduce_d(1, 1)
        if j > 1:
            gather_own(j + 2)
        if j > 2:
            reduce_b(j - 1, 1)
        if j == 3:
            reduce_o(1, 1)
            reduce_b(1, 1)
        second_product(j, wide, 3 * wide // 2)
        if j > 1:
            gather_last(j + 1)
        second_product(j, 3 * wide // 2, 2 * wide)
        start(j, PAIR + 1)
        if j == 0:
            gather_last(1)
        if j > 1 and j < last:
            reduce_a(j, 0)
        if j > 2:
            reduce_c(j - 1, 0)
            if j < last:
                reduce_c(j - 1, 1)
    reduce_a(last, 0)
    if last > 2:
        reduce_c(last - 1, 1)
    reduce_d(last, 1)
    reduce_o(0, 0)
    reduce_c(1, 0)
    reduce_b(last, 0)
    reduce_o(last, 1)
    reduce_b(last, 1)
    reduce_c(1, 1)
    reduce_d(0, 1)
    reduce_c(last, 0)
    reduce_o(0, 1)
    reduce_b(0, 0)
    reduce_c(last, 1)
    reduce_b(0, 1)
    reduce_c(0, 0)
    reduce_c(0, 1)

    turned = (((1,), (1,)), ((), ()))
    same = jnp.where(row_at == col_at, 1.0, 0.0)
    earlier = jnp.where(col_at < row_at, 1.0, 0.0).astype(BF16)
    named = lax.dot_general(same.astype(BF16), named_t, turned, preferred_element_type=F32)
    rank = lax.dot_general(earlier, named_t, turned, preferred_element_type=F32)
    gatest = gatest_ref[...]
    shares_t = jnp.where(first, gatest[0:1, :], 0.0) + jnp.where(second, gatest[1:2, :], 0.0)
    shares = lax.dot_general(
        same, shares_t, turned, preferred_element_type=F32, precision=lax.Precision.HIGHEST
    )
    place = lax.broadcasted_iota(jnp.int32, (tok, cap), 1).astype(F32)
    gives = []
    for j in range(experts):
        pick = (rank[:, j : j + 1] == place) & (named[:, j : j + 1] > 0.5)
        gives.append(jnp.where(pick, 1.0, 0.0).astype(BF16))
    for j in range(1, experts):
        arrived(j, BACK, BACK + 1)
    for n in range(width // 512):
        at = slice(n * 512, (n + 1) * 512)
        mixed = tokens_ref[:, at].astype(F32)
        for j in range(experts):
            value = jnp.dot(gives[j], returned[j, :, at], preferred_element_type=F32)
            mixed = mixed + shares[:, j : j + 1] * (value + b_out_ref[pl.ds(planes[j], 1), at])
        out_ref[:, at] = mixed.astype(BF16)
    for each in copies.values():
        each.wait_send()


def local(tokens, expert_ids, gate_weights, norm_gain, norm_bias, w_in, b_in, w_out, b_out):
    tok, width = tokens.shape
    top = expert_ids.shape[1]
    devices = lax.axis_size("local")
    experts = b_out.shape[0]
    shared = devices // experts
    hid = b_in.shape[1]
    cap = min(tok, shared * max(1, (3 * tok * top // (2 * experts) + shared - 1) // shared))
    cap = -(-cap // 16) * 16
    vmem = pl.BlockSpec(memory_space=pltpu.VMEM)
    hbm = pl.BlockSpec(memory_space=pl.ANY)
    return pl.pallas_call(
        functools.partial(kernel, experts, cap),
        out_shape=jax.ShapeDtypeStruct((tok, width), BF16),
        in_specs=[vmem] * 7 + [hbm] * 2,
        out_specs=vmem,
        scratch_shapes=[
            pltpu.VMEM((width, hid), BF16),
            pltpu.VMEM((hid, width), BF16),
            pltpu.VMEM((experts, 8 * cap, width), BF16),
            pltpu.VMEM((experts, cap, width), BF16),
            pltpu.VMEM((8 * cap, hid), BF16),
            pltpu.VMEM((experts, 8 * cap, width), BF16),
            pltpu.VMEM((experts, 4 * cap, width), BF16),
            pltpu.VMEM((experts, cap, width), BF16),
            pltpu.VMEM((experts, cap, width), BF16),
            pltpu.VMEM((experts, cap, width), BF16),
            pltpu.VMEM((experts, 3, cap, width), BF16),
            pltpu.VMEM((experts, cap, width), BF16),
            pltpu.VMEM((experts, cap, width), BF16),
            pltpu.SemaphoreType.DMA((2,)),
            pltpu.SemaphoreType.DMA((experts * KINDS,)),
            pltpu.SemaphoreType.DMA((experts * KINDS,)),
        ],
        compiler_params=pltpu.CompilerParams(
            collective_id=0, has_side_effects=True, vmem_limit_bytes=64 * 1024 * 1000
        ),
    )(
        tokens, expert_ids.T, gate_weights.T, norm_gain[None, :], norm_bias[None, :], b_in, b_out, w_in, w_out,
    )


def solution(mesh):
    in_specs = (
        P(("groups", "local"), None),
        P(("groups", "local"), None),
        P(("groups", "local"), None),
        P(),
        P(),
        P("local", None, None),
        P("local", None),
        P("local", None, None),
        P(),
    )
    out_specs = P(("groups", "local"), None)
    return jax.shard_map(local, mesh=mesh, in_specs=in_specs, out_specs=out_specs, check_vma=False)
```
